32 devices in a mesh: row: 4 (over y, x), col: 8 (over z, core).
Axes of the slice: x: 2, y: 2, z: 4, core: 2. Of those that a mesh axis runs over, the one named last changes fastest.
Arguments:
- halves: float32 [2, 2048, 8192], P(None, 'row', 'col'), may hold values from -6 to 6
- diag_rest: float32 [4096, 1024], P(('col', 'row')), may hold values from -6 to 6
- panel_vectors: float32 [8192, 256], P('col'), may hold values from -1 to 1
- tri_factor: float32 [256, 256], replicated, may hold values from -1 to 2, as said below
Outputs:
- updated_halves: float32 [2, 2048, 8192], P(None, 'row', 'col')
- updated_rest: float32 [4096, 1024], P(('col', 'row'))
- w_panel: float32 [8192, 256], P('col')
The draws below stay inside these ranges and needn't reach their ends.
Inputs may be any that keep to these rules, and one draw needn't show every extreme that they name: `tri_factor`: upper triangular, diagonal between 1 and 2.
All inputs are finite; a program needn't handle non-finite values.
Results may differ from the reference program's by a relative error of at most 0.0003.
Values sent between devices are 32-bit elements; how exact they have to be, the bound alone decides.
No kernel may reach another device: no remote copies, remote signals or barrier semaphores. Data moves between devices by JAX's collectives and lax.ppermute only.
A program may use at most 64 MiB of HBM per device.

```python
import jax
import jax.numpy as jnp
from jax import lax

TILE = 1024
K = 256
ORDER = 8192
N_ROW = 4
N_COL = 8


def draw_panel_vectors(key, part):
    base = jax.random.normal(key, (ORDER, K), jnp.float32)
    basis, upper = jnp.linalg.qr(base)
    return basis


def draw_tri_factor(key, part):
    first, second = jax.random.split(jax.random.fold_in(key, 7))
    spread = jnp.clip(jax.random.normal(first, (K, K), jnp.float32), -4.0, 4.0) / K ** 0.5
    diagonal = jax.random.uniform(second, (K,), jnp.float32, minval=1.0, maxval=2.0)
    return jnp.triu(spread, 1) + jnp.diag(diagonal)


def block_levels(stream_key, dims, cuts, low, largest):
    factor_of, own = 1.0, jax.random.fold_in(stream_key, 6)
    for axis_at, parts in cuts:
        steps = jnp.exp(jax.random.uniform(jax.random.fold_in(own, axis_at), (parts,), jnp.float32, low / len(cuts), largest / len(cuts)))
        factor_of = factor_of * jnp.repeat(steps, dims[axis_at] // parts).reshape([-1 if axis == axis_at else 1 for axis in range(len(dims))])
    return factor_of


def scatter_about(rng, extent, deviation, reach, pieces=(), kind=jnp.bfloat16):
    values = jax.random.normal(rng, extent, jnp.float32) * deviation
    if len(pieces) > 0:
        values = block_levels(rng, extent, pieces, -0.22, 0.18) * values
    return jnp.clip(values, min=-reach, max=reach).astype(kind)


def setup_inputs(seed: int = 0) -> dict:
    key_list = jax.random.split(jax.random.key(seed), 5)
    halves = scatter_about(key_list[0], (2, N_ROW * TILE // 2, ORDER), 1.0, 6.0, ((1, 4), (2, 8)), jnp.float32)
    diag_rest = scatter_about(key_list[1], (ORDER // 2, TILE), 1.0, 6.0, ((0, 32),), jnp.float32)
    panel_vectors = draw_panel_vectors(jax.random.fold_in(key_list[4], 71), 0)
    tri_factor = draw_tri_factor(jax.random.fold_in(key_list[4], 71), 0)
    return {"halves": halves, "diag_rest": diag_rest, "panel_vectors": panel_vectors, "tri_factor": tri_factor}


precise = lax.Precision.HIGHEST

def reference(halves, diag_rest, panel_vectors, tri_factor):
    blocks = N_COL
    half_size = TILE // 2
    stored = halves.reshape(2, N_ROW, half_size, blocks, TILE).transpose(0, 1, 3, 2, 4).reshape(blocks, blocks, half_size, TILE)
    vectors = panel_vectors.reshape(blocks, TILE, K)
    vec_halves = vectors.reshape(blocks, 2, half_size, K)
    rest = diag_rest.reshape(blocks, half_size, TILE)
    index = jnp.arange(blocks, dtype=jnp.int32)

    def geometry(block_row):
        is_lower = block_row >= index
        low_block = jnp.minimum(block_row, index).astype(jnp.int32)
        high_block = jnp.maximum(block_row, index).astype(jnp.int32)
        which = jnp.where(is_lower, 0, 1).astype(jnp.int32)
        weight = jnp.where(block_row == index, 0.5, 1.0).astype(jnp.float32)
        return (is_lower, low_block, high_block, which, weight)

    def add_terms(block_row, total):
        is_lower, low_block, high_block, which, weight = geometry(block_row)
        tiles = stored[block_row]
        low_vec = vectors[low_block]
        high_half = vec_halves[high_block, which]
        first = jnp.einsum('qhT,qTk->qhk', tiles, low_vec, precision=precise) * weight[:, None, None]
        second = jnp.einsum('qhT,qhk->qTk', tiles, high_half, precision=precise) * weight[:, None, None]
        zeros = jnp.zeros_like(first)
        padded = jnp.where(is_lower[:, None, None], jnp.concatenate([first, zeros], 1), jnp.concatenate([zeros, first], 1))
        one_high = (high_block[:, None] == index[None, :]).astype(jnp.float32)
        one_low = (low_block[:, None] == index[None, :]).astype(jnp.float32)
        total = total + jnp.einsum('qi,qTk->iTk', one_high, padded, precision=precise)
        return total + jnp.einsum('qi,qTk->iTk', one_low, second, precision=precise)
    total = lax.fori_loop(0, blocks, add_terms, jnp.zeros((blocks, TILE, K), jnp.float32))
    first_rest = jnp.einsum('ihT,iTk->ihk', rest, vectors, precision=precise) * 0.5
    second_rest = jnp.einsum('ihT,ihk->iTk', rest, vec_halves[:, 1], precision=precise) * 0.5
    av_blocks = total + jnp.concatenate([jnp.zeros_like(first_rest), first_rest], 1) + second_rest
    inner = jnp.einsum('iTk,iTl->kl', vectors, av_blocks, precision=precise)
    middle = jnp.dot(jnp.dot(tri_factor.T, inner, precision=precise), tri_factor, precision=precise)
    w_blocks = jnp.einsum('iTk,kl->iTl', av_blocks, tri_factor, precision=precise) - 0.5 * jnp.einsum('iTk,kl->iTl', vectors, middle, precision=precise)
    w_halves = w_blocks.reshape(blocks, 2, half_size, K)

    def update_row(block_row):
        is_lower, low_block, high_block, which, weight = geometry(block_row)
        left = jnp.concatenate([vec_halves[high_block, which], w_halves[high_block, which]], -1)
        right = jnp.concatenate([w_blocks[low_block], vectors[low_block]], -1)
        return stored[block_row] - jnp.einsum('qhk,qTk->qhT', left, right, precision=precise)
    new_stored = lax.map(update_row, index)
    new_halves = new_stored.reshape(2, N_ROW, blocks, half_size, TILE).transpose(0, 1, 3, 2, 4).reshape(2, N_ROW * half_size, blocks * TILE)
    left_rest = jnp.concatenate([vec_halves[:, 1], w_halves[:, 1]], -1)
    right_rest = jnp.concatenate([w_blocks, vectors], -1)
    new_rest = rest - jnp.einsum('ihk,iTk->ihT', left_rest, right_rest, precision=precise)
    return (new_halves, new_rest.reshape(blocks * half_size, TILE), w_blocks.reshape(blocks * TILE, K))
```

```python
import jax
import jax.numpy as jnp
from jax import lax
from jax.sharding import PartitionSpec as P

high = lax.Precision.HIGH


def matmul(left, right):
    return jnp.dot(left, right, precision=high, preferred_element_type=jnp.float32)


def left_contract(left, right):
    return lax.dot_general(
        left, right, (((0,), (0,)), ((), ())), precision=high, preferred_element_type=jnp.float32
    )


def right_contract(left, right):
    return lax.dot_general(
        left, right, (((1,), (1,)), ((), ())), precision=high, preferred_element_type=jnp.float32
    )


class Routes:
    def __init__(self, rows, cols):
        self.rows, self.cols = rows, cols
        self.planes = cols // 2
        self.top = rows // 2

    def flat(self, row, col):
        return row * self.cols + col

    def send(self, value, pairs):
        return lax.ppermute(value, ("row", "col"), pairs)

    def across_rows(self, bit):
        return [
            (self.flat(r, c), self.flat(r ^ bit, c))
            for r in range(self.rows)
            for c in range(self.cols)
        ]

    def across_cols(self, bit):
        return [
            (self.flat(r, c), self.flat(r, c ^ bit))
            for r in range(self.rows)
            for c in range(self.cols)
        ]

    def collector(self, block):
        return block % 2 if block < self.rows else 1 - block % 2

    def trips(self, step):
        pairs = []
        for block in range(self.cols):
            home = block // 2
            row = block % self.rows
            for away in range(1, self.planes):
                plane = (home + away) % self.planes
                there = self.flat(row, 2 * plane + self.collector(block))
                if away - 1 == step:
                    pairs.append((self.flat(row, block), there))
                if away % (self.planes - 1) == step and plane > home:
                    pairs.append((self.flat(row ^ self.top, block), there))
        return pairs

    def spread(self, half):
        return [self.send(half, self.trips(step)) for step in range(self.planes - 1)]


def shards(halves, diag_rest, panel_vectors, tri_factor):
    rows, cols = lax.axis_size("row"), lax.axis_size("col")
    routes = Routes(rows, cols)
    planes, top = routes.planes, routes.top
    row, col = lax.axis_index("row"), lax.axis_index("col")
    half_size, tile_size = halves.shape[1:]
    width = panel_vectors.shape[1]
    rest_rows = diag_rest.shape[0]
    rest_start = half_size + row * rest_rows
    core, plane = col % 2, col // 2
    owner = col % rows
    first_panel = core == row % 2
    mine = jnp.where(first_panel, row, row + rows)
    away = (plane - mine // 2) % planes
    swap = routes.across_cols(1)

    def half(panel, index):
        return lax.dynamic_slice_in_dim(panel, index * half_size, half_size, 0)

    def assemble(base, arrived):
        upper = lax.select_n(away, base[:half_size], *arrived)
        shifted = [arrived[-1]] + arrived[:-1]
        shifted = [arrived[(step + 1) % (planes - 1)] for step in range(planes - 1)]
        lower = lax.select_n(away, base[half_size:], *shifted)
        return jnp.concatenate([upper, lower], 0)

    lane = jnp.where(row == owner, 0, 1)
    arrived = routes.spread(half(panel_vectors, lane))
    partner = routes.send(panel_vectors, swap)
    mine_vec = assemble(jnp.where(mine == col, panel_vectors, partner), arrived)
    other_vec = routes.send(mine_vec, swap)
    row_vecs = [jnp.where(first_panel, mine_vec, other_vec), jnp.where(first_panel, other_vec, mine_vec)]

    zero_half = jnp.zeros((half_size, width), jnp.float32)
    row_parts, lowers, weights = [], [], []
    for position in range(2):
        block_row = row + rows * position
        is_lower = block_row >= col
        weight = jnp.where(block_row == col, 0.5, 1.0).astype(jnp.float32)
        row_parts.append(
            lax.cond(
                is_lower,
                lambda tile: jnp.concatenate([matmul(tile, panel_vectors) * weight, zero_half], 0),
                lambda tile: left_contract(tile, panel_vectors[half_size:]),
                halves[position],
            )
        )
        lowers.append(is_lower)
        weights.append(weight)
    kept = jnp.where(first_panel, row_parts[0], row_parts[1])
    given = jnp.where(first_panel, row_parts[1], row_parts[0])
    chip_sum = kept + routes.send(given, swap)
    row_sums = []
    for step in range(planes - 1):
        back = [(there, here) for here, there in routes.trips(step)]
        part = jnp.where(away == step + 1, chip_sum[:half_size], chip_sum[half_size:])
        row_sums.append(routes.send(part, back))
    home = [
        (routes.flat(b % rows, b ^ 1), routes.flat(b % rows, b)) for b in range(rows, cols)
    ]
    col_part = jnp.where(mine == col, chip_sum, routes.send(chip_sum, home))

    own_rest_vec = lax.dynamic_slice_in_dim(panel_vectors, rest_start, rest_rows, 0)
    rest_first = 0.5 * matmul(diag_rest, panel_vectors)
    col_part = col_part + 0.5 * left_contract(diag_rest, own_rest_vec)
    col_part = lax.dynamic_update_slice_in_dim(
        col_part,
        lax.dynamic_slice_in_dim(col_part, rest_start, rest_rows, 0) + rest_first,
        rest_start,
        0,
    )
    inner = left_contract(own_rest_vec, rest_first)

    for position in range(2):
        weight = weights[position]

        def below(tile, vec, weight=weight, position=position):
            part = left_contract(tile, vec[:half_size]) * weight
            return part, left_contract(vec[:half_size], row_parts[position][:half_size])

        def above(tile, vec):
            part = matmul(tile, vec)
            return jnp.concatenate([zero_half, part], 0), left_contract(panel_vectors[half_size:], part)

        part, cross = lax.cond(lowers[position], below, above, halves[position], row_vecs[position])
        col_part = col_part + part
        inner = inner + cross
    inner = inner + inner.T

    moved = jnp.where((row ^ owner) & top == 0, 1, 0)
    sent, stays = half(col_part, moved), half(col_part, 1 - moved)
    bit = top // 2
    while bit >= 1:
        pairs = [
            (routes.flat(r, c), routes.flat(r ^ bit, c))
            for r in range(rows)
            for c in range(cols)
            if (r ^ (c % rows)) & bit and (r ^ (c % rows)) % top // (2 * bit) == 0
        ]
        sent, stays = sent + routes.send(sent, pairs), stays + routes.send(stays, pairs)
        bit //= 2
    lanes = [
        (routes.flat(r, c), routes.flat(r ^ top, c))
        for r in range(rows)
        for c in range(cols)
        if (r ^ (c % rows)) % top == 0
    ]
    total = stays + routes.send(sent, lanes)
    for row_sum in row_sums:
        total = total + row_sum

    arrived = routes.spread(total)
    beside = [None]
    for step in range(1, rows):
        pairs = [
            (routes.flat(r, c), routes.flat(r ^ step, c))
            for r in range(rows)
            for c in range(cols)
            if (r ^ (c % rows)) % top == 0
        ]
        beside.append(routes.send(total, pairs))
    apart = row ^ owner
    upper = lax.select_n(apart, total, *beside[1:])
    lower = lax.select_n(apart, *[total if q == top else beside[q ^ top] for q in range(rows)])
    own_av = jnp.concatenate([upper, lower], 0)

    bit = 1
    while bit < cols:
        inner = inner + routes.send(inner, routes.across_cols(bit))
        bit *= 2
    bit = 1
    while bit < rows:
        inner = inner + routes.send(inner, routes.across_rows(bit))
        bit *= 2
    half_middle = 0.5 * matmul(left_contract(tri_factor, inner), tri_factor)

    own_w = matmul(own_av, tri_factor) - matmul(panel_vectors, half_middle)
    partner_w = routes.send(own_w, swap)
    mine_av = assemble(own_av, arrived)
    mine_w = matmul(mine_av, tri_factor) - matmul(mine_vec, half_middle)
    mine_w = jnp.where(mine == (col ^ 1), partner_w, mine_w)
    other_w = routes.send(mine_w, swap)
    row_ws = [jnp.where(first_panel, mine_w, other_w), jnp.where(first_panel, other_w, mine_w)]

    updated = []
    for position in range(2):
        vec, w = row_vecs[position], row_ws[position]
        is_lower = lowers[position]
        low_vec = jnp.where(is_lower, panel_vectors, vec)
        low_w = jnp.where(is_lower, own_w, w)
        high_vec = jnp.where(is_lower, vec[:half_size], panel_vectors[half_size:])
        high_w = jnp.where(is_lower, w[:half_size], own_w[half_size:])
        left = jnp.concatenate([high_vec, high_w], 1)
        right = jnp.concatenate([low_w, low_vec], 1)
        updated.append(halves[position] - right_contract(left, right))
    own_rest_w = lax.dynamic_slice_in_dim(own_w, rest_start, rest_rows, 0)
    left_rest = jnp.concatenate([own_rest_vec, own_rest_w], 1)
    right_rest = jnp.concatenate([own_w, panel_vectors], 1)
    new_rest = diag_rest - right_contract(left_rest, right_rest)
    return (jnp.stack(updated), new_rest, own_w)


def solution(mesh):
    return jax.shard_map(
        shards,
        mesh=mesh,
        in_specs=(P(None, "row", "col"), P(("col", "row"), None), P("col", None), P()),
        out_specs=(P(None, "row", "col"), P(("col", "row"), None), P("col", None)),
        check_vma=False,
    )
```

```python
import functools

import jax
import jax.numpy as jnp
from jax import lax
from jax.experimental import pallas as pl
from jax.experimental.pallas import tpu as pltpu
from jax.sharding import PartitionSpec as P

f32, bf16 = jnp.float32, jnp.bfloat16

ANY = pl.BlockSpec(memory_space=pl.ANY)


def split(value):
    top = value.astype(bf16)
    return top, (value - top.astype(f32)).astype(bf16)


def product(left, right, dims):
    def term(a, b):
        return lax.dot_general(a, b, (dims, ((), ())), preferred_element_type=f32)

    return term(left[0], right[0]) + (term(left[0], right[1]) + term(left[1], right[0]))


NN = ((1,), (0,))
TN = ((0,), (0,))
NT = ((1,), (1,))


class Routes:
    def __init__(self, rows, cols):
        self.rows, self.cols = rows, cols
        self.planes = cols // 2
        self.top = rows // 2

    def flat(self, row, col):
        return row * self.cols + col

    def send(self, value, pairs):
        return lax.ppermute(value, ("row", "col"), pairs)

    def across_rows(self, bit):
        return [
            (self.flat(r, c), self.flat(r ^ bit, c))
            for r in range(self.rows)
            for c in range(self.cols)
        ]

    def across_cols(self, bit):
        return [
            (self.flat(r, c), self.flat(r, c ^ bit))
            for r in range(self.rows)
            for c in range(self.cols)
        ]

    def collector(self, block):
        return block % 2 if block < self.rows else 1 - block % 2

    def trips(self, step):
        pairs = []
        for block in range(self.cols):
            home = block // 2
            row = block % self.rows
            for away in range(1, self.planes):
                plane = (home + away) % self.planes
                there = self.flat(row, 2 * plane + self.collector(block))
                if away - 1 == step:
                    pairs.append((self.flat(row, block), there))
                if away % (self.planes - 1) == step and plane > home:
                    pairs.append((self.flat(row ^ self.top, block), there))
        return pairs

    def spread(self, half):
        return [self.send(half, self.trips(step)) for step in range(self.planes - 1)]


class Place:
    def __init__(self, rows, cols):
        self.rows = rows
        self.row, self.col = lax.axis_index("row"), lax.axis_index("col")
        self.planes, self.top = cols // 2, rows // 2
        self.first_panel = lax.rem(self.col, 2) == lax.rem(self.row, 2)
        self.mine = jnp.where(self.first_panel, self.row, self.row + rows)
        self.other = jnp.where(self.first_panel, self.row + rows, self.row)
        self.my_position = jnp.where(self.first_panel, 0, 1)
        self.away = lax.rem(self.col // 2 - self.mine // 2 + self.planes, self.planes)
        self.apart = self.row ^ lax.rem(self.col, rows)


def pick(choices, target, sem):
    for condition, source in choices:
        @pl.when(condition)
        def _(source=source):
            pltpu.make_async_copy(source, target, sem).start()

    return pltpu.make_async_copy(choices[0][1], target, sem)


def load(source, target, sem):
    copy = pltpu.make_async_copy(source, target, sem)
    copy.start()
    return copy


def kernel_call(body, args, outs, scratch, flops=0, moved=0, aliases=None):
    return pl.pallas_call(
        body,
        out_shape=outs,
        in_specs=[ANY] * len(args),
        out_specs=jax.tree.map(lambda _: ANY, outs),
        scratch_shapes=scratch,
        input_output_aliases=aliases or {},
        cost_estimate=pl.CostEstimate(flops=flops, bytes_accessed=moved, transcendentals=0),
        compiler_params=pltpu.CompilerParams(vmem_limit_bytes=32 * 2**20),
    )(*args)


def row_kernel(rows, cols, halves, rest, vec, kept, given, around, cross, tiles, panel, rest_v, parts, total, square, sems):
    at = Place(rows, cols)
    half = tiles.shape[1]
    rest_rows = rest_v.shape[0]
    loads = [
        load(vec, panel, sems.at[0]),
        load(halves.at[0], tiles.at[0], sems.at[1]),
        load(halves.at[1], tiles.at[1], sems.at[2]),
        load(rest, rest_v, sems.at[3]),
    ]
    loads[0].wait()
    local = split(panel[...])
    for position in range(2):
        loads[1 + position].wait()
        block_row = at.row + rows * position
        tile = split(tiles[position])

        @pl.when(block_row >= at.col)
        def _(tile=tile, position=position, block_row=block_row):
            weight = jnp.where(block_row == at.col, 0.5, 1.0).astype(f32)
            parts[position, :half] = product(tile, local, NN) * weight
            parts[position, half:] = jnp.zeros((half, panel.shape[1]), f32)

        @pl.when(block_row < at.col)
        def _(tile=tile, position=position):
            parts[position] = product(tile, (local[0][half:], local[1][half:]), TN)

    keeps = load(parts.at[at.my_position], kept, sems.at[4])
    gives = load(parts.at[1 - at.my_position], given, sems.at[5])
    loads[3].wait()
    start = pl.multiple_of(half + at.row * rest_rows, rest_rows)
    mine = split(rest_v[...])
    total[...] = 0.5 * product(mine, split(panel[pl.ds(start, rest_rows), :]), TN)
    total[pl.ds(start, rest_rows), :] += 0.5 * product(mine, local, NN)
    square[...] = product(local, split(total[...]), TN)
    last = [load(total, around, sems.at[6]), load(square, cross, sems.at[7])]
    for copy in [keeps, gives] + last:
        copy.wait()


def row_products(rows, cols, halves, rest, vec):
    half, tile = halves.shape[1:]
    width = vec.shape[1]
    panel = jax.ShapeDtypeStruct((tile, width), f32)
    return kernel_call(
        functools.partial(row_kernel, rows, cols),
        (halves, rest, vec),
        (panel, panel, panel, jax.ShapeDtypeStruct((width, width), f32)),
        [
            pltpu.VMEM(halves.shape, f32),
            pltpu.VMEM(vec.shape, f32),
            pltpu.VMEM(rest.shape, f32),
            pltpu.VMEM((2, tile, width), f32),
            pltpu.VMEM((tile, width), f32),
            pltpu.VMEM((width, width), f32),
            pltpu.SemaphoreType.DMA((8,)),
        ],
        3 * 5 * half * tile * width,
        4 * (2 * halves.size + 5 * vec.size),
    )


def assemble_kernel(rows, cols, own, partner, *refs):
    arrived, out, panel, sems = refs[:-3], refs[-3], refs[-2], refs[-1]
    at = Place(rows, cols)
    half = panel.shape[0] // 2
    steps = at.planes - 1
    for index in range(2):
        piece = pl.ds(index * half, half)
        choices = [
            ((at.away == 0) & (at.mine == at.col), own.at[piece]),
            ((at.away == 0) & (at.mine != at.col), partner.at[piece]),
        ]
        for away in range(1, at.planes):
            step = away - 1 if index == 0 else away % steps
            choices.append((at.away == away, arrived[step]))
        pick(choices, panel.at[piece], sems.at[index]).wait()
    load(panel, out, sems.at[2]).wait()


def assemble(rows, cols, own, partner, arrived):
    return kernel_call(
        functools.partial(assemble_kernel, rows, cols),
        (own, partner, *arrived),
        jax.ShapeDtypeStruct(own.shape, f32),
        [pltpu.VMEM(own.shape, f32), pltpu.SemaphoreType.DMA((3,))],
        0,
        8 * own.size,
    )


def column_part(at, position, tiles, panel, total, half):
    block_row = at.row + at.rows * position

    @pl.when(block_row >= at.col)
    def _():
        weight = jnp.where(block_row == at.col, 0.5, 1.0).astype(f32)
        total[...] += product(split(tiles[...]), split(panel[:half]), TN) * weight

    @pl.when(block_row < at.col)
    def _():
        total[half:] += product(split(tiles[...]), split(panel[...]), NN)


def first_column_kernel(rows, cols, halves, vec, out, tiles, panel, total, sems):
    at = Place(rows, cols)
    loads = [load(vec, panel, sems.at[0]), load(halves.at[at.my_position], tiles, sems.at[1])]
    total[...] = jnp.zeros(total.shape, f32)
    for copy in loads:
        copy.wait()
    column_part(at, at.my_position, tiles, panel, total, tiles.shape[0])
    load(total, out, sems.at[2]).wait()


def second_column_kernel(
    rows, cols, halves, vec, own, partial, around, cross, sum_own, sum_partner, sent, stays, inner,
    tiles, panel, local, total, extra, square, sems,
):
    at = Place(rows, cols)
    half = tiles.shape[0]
    loads = [
        load(partial, total, sems.at[0]),
        load(vec, panel, sems.at[1]),
        load(halves.at[1 - at.my_position], tiles, sems.at[2]),
        load(own, local, sems.at[3]),
        load(around, extra.at[0], sems.at[4]),
        load(cross, square, sems.at[5]),
    ]
    theirs = at.other == at.col
    ours = at.mine == at.col
    sums = pick([(theirs, sum_partner), (jnp.logical_not(theirs), sum_own)], extra.at[1], sems.at[6])
    for copy in loads[:3]:
        copy.wait()
    column_part(at, 1 - at.my_position, tiles, panel, total, half)
    loads[3].wait()
    loads[5].wait()
    flat = product(split(local[...]), split(total[...]), TN)
    square[...] += flat + flat.T
    loads[4].wait()
    sums.wait()
    used = jnp.where(theirs | ours, 1.0, 0.0).astype(f32)
    total[...] += extra[0] + used * extra[1]
    moved = jnp.where(at.apart & at.top == 0, 1, 0)
    outs = [
        load(total.at[pl.ds(pl.multiple_of(moved * half, half), half)], sent, sems.at[7]),
        load(total.at[pl.ds(pl.multiple_of((1 - moved) * half, half), half)], stays, sems.at[8]),
        load(square, inner, sems.at[9]),
    ]
    for copy in outs:
        copy.wait()


def first_column(rows, cols, halves, vec):
    half, tile = halves.shape[1:]
    return kernel_call(
        functools.partial(first_column_kernel, rows, cols),
        (halves, vec),
        jax.ShapeDtypeStruct(vec.shape, f32),
        [
            pltpu.VMEM((half, tile), f32),
            pltpu.VMEM(vec.shape, f32),
            pltpu.VMEM(vec.shape, f32),
            pltpu.SemaphoreType.DMA((3,)),
        ],
        6 * half * vec.size,
        2 * halves.size,
    )


def second_column(rows, cols, halves, vec, own, partial, around, cross, sum_own, sum_partner):
    half, tile = halves.shape[1:]
    width = vec.shape[1]
    piece = jax.ShapeDtypeStruct((half, width), f32)
    return kernel_call(
        functools.partial(second_column_kernel, rows, cols),
        (halves, vec, own, partial, around, cross, sum_own, sum_partner),
        (piece, piece, jax.ShapeDtypeStruct((width, width), f32)),
        [
            pltpu.VMEM((half, tile), f32),
            pltpu.VMEM(vec.shape, f32),
            pltpu.VMEM(vec.shape, f32),
            pltpu.VMEM(vec.shape, f32),
            pltpu.VMEM((2, *vec.shape), f32),
            pltpu.VMEM((width, width), f32),
            pltpu.SemaphoreType.DMA((10,)),
        ],
        6 * half * vec.size,
        2 * halves.size + 20 * vec.size,
    )


def own_kernel(rows, cols, vec, tri, inner, rest, total, *refs):
    beside = refs[: rows - 1]
    w_out, half_middle, rest_out, panel, factor, square, av, w, rest_v, sems = refs[rows - 1 :]
    at = Place(rows, cols)
    half = total.shape[0]
    rest_rows = rest_v.shape[0]
    loads = [
        load(inner, square, sems.at[0]),
        load(tri, factor, sems.at[1]),
        load(vec, panel, sems.at[2]),
        load(rest, rest_v, sems.at[3]),
    ]
    sources = [total, *beside]
    halves_of = []
    for index in range(2):
        choices = []
        for apart in range(rows):
            come = apart if index == 0 else apart ^ at.top
            choices.append((at.apart == apart, sources[come]))
        halves_of.append(pick(choices, av.at[pl.ds(index * half, half)], sems.at[4 + index]))
    loads[0].wait()
    loads[1].wait()
    split_factor = split(factor[...])
    square[...] = 0.5 * product(split(product(split_factor, split(square[...]), TN)), split_factor, NN)
    middle_copy = load(square, half_middle, sems.at[6])
    loads[2].wait()
    for copy in halves_of:
        copy.wait()
    w[...] = product(split(av[...]), split_factor, NN) - product(split(panel[...]), split(square[...]), NN)
    w_copy = load(w, w_out, sems.at[7])
    loads[3].wait()
    start = pl.multiple_of(half + at.row * rest_rows, rest_rows)
    left_v, left_w = split(panel[pl.ds(start, rest_rows), :]), split(w[pl.ds(start, rest_rows), :])
    rest_v[...] -= product(left_v, split(w[...]), NT) + product(left_w, split(panel[...]), NT)
    load(rest_v, rest_out, sems.at[8]).wait()
    middle_copy.wait()
    w_copy.wait()


def own_w_and_rest(rows, cols, vec, tri, inner, rest, total, beside):
    width = vec.shape[1]
    square = jax.ShapeDtypeStruct((width, width), f32)
    return kernel_call(
        functools.partial(own_kernel, rows, cols),
        (vec, tri, inner, rest, total, *beside),
        (jax.ShapeDtypeStruct(vec.shape, f32), square, jax.ShapeDtypeStruct(rest.shape, f32)),
        [
            pltpu.VMEM(vec.shape, f32),
            pltpu.VMEM((width, width), f32),
            pltpu.VMEM((width, width), f32),
            pltpu.VMEM(vec.shape, f32),
            pltpu.VMEM(vec.shape, f32),
            pltpu.VMEM(rest.shape, f32),
            pltpu.SemaphoreType.DMA((9,)),
        ],
        15 * width * vec.size,
        16 * vec.size,
    )


def mine_kernel(rows, cols, vec, tri, middle, own_w, partner_w, *refs):
    arrived = refs[: cols // 2 - 1]
    out, panel, factor, square, av, sems = refs[cols // 2 - 1 :]
    at = Place(rows, cols)
    half = panel.shape[0] // 2
    steps = at.planes - 1
    home = at.away == 0
    loads = [load(middle, square, sems.at[0]), load(tri, factor, sems.at[1]), load(vec, panel, sems.at[2])]
    waits = []
    for index in range(2):
        piece = pl.ds(index * half, half)
        choices = [
            (home & (at.mine == at.col), own_w.at[piece]),
            (home & (at.mine != at.col), partner_w.at[piece]),
        ]
        for away in range(1, at.planes):
            step = away - 1 if index == 0 else away % steps
            choices.append((at.away == away, arrived[step]))
        waits.append(pick(choices, av.at[piece], sems.at[3 + index]))
    for copy in loads + waits:
        copy.wait()

    @pl.when(jnp.logical_not(home))
    def _():
        av[...] = product(split(av[...]), split(factor[...]), NN) - product(
            split(panel[...]), split(square[...]), NN
        )

    load(av, out, sems.at[5]).wait()


def mine_w_panel(rows, cols, vec, tri, middle, own_w, partner_w, arrived):
    width = vec.shape[1]
    return kernel_call(
        functools.partial(mine_kernel, rows, cols),
        (vec, tri, middle, own_w, partner_w, *arrived),
        jax.ShapeDtypeStruct(vec.shape, f32),
        [
            pltpu.VMEM(vec.shape, f32),
            pltpu.VMEM((width, width), f32),
            pltpu.VMEM((width, width), f32),
            pltpu.VMEM(vec.shape, f32),
            pltpu.SemaphoreType.DMA((6,)),
        ],
        12 * width * vec.size,
        12 * vec.size,
    )


def update_kernel(rows, cols, which, halves, own_v, own_w, row_v, row_w, *refs):
    out, tiles, left, right, sems = refs[-5:]
    at = Place(rows, cols)
    half, width = left.shape[1:]
    position = at.my_position if which == 0 else 1 - at.my_position
    is_lower = at.row + rows * position >= at.col
    is_upper = jnp.logical_not(is_lower)
    bottom = pl.ds(half, half)
    top = pl.ds(0, half)
    waits = [
        pick([(is_lower, row_v.at[top]), (is_upper, own_v.at[bottom])], left.at[0], sems.at[0]),
        pick([(is_lower, row_w.at[top]), (is_upper, own_w.at[bottom])], left.at[1], sems.at[1]),
        pick([(is_lower, own_w), (is_upper, row_w)], right.at[0], sems.at[2]),
        pick([(is_lower, own_v), (is_upper, row_v)], right.at[1], sems.at[3]),
        load(halves.at[position], tiles, sems.at[4]),
    ]
    for copy in waits:
        copy.wait()
    lefts = [split(left[index]) for index in range(2)]
    rights = [split(right[index]) for index in range(2)]
    tiles[...] -= product(lefts[0], rights[0], NT) + product(lefts[1], rights[1], NT)
    load(tiles, out.at[position], sems.at[5]).wait()


def update(rows, cols, which, halves, own_v, own_w, row_v, row_w, before=None):
    half, tile = halves.shape[1:]
    width = own_v.shape[1]
    args = (halves, own_v, own_w, row_v, row_w) + (() if before is None else (before,))
    return kernel_call(
        functools.partial(update_kernel, rows, cols, which),
        args,
        jax.ShapeDtypeStruct(halves.shape, f32),
        [
            pltpu.VMEM((half, tile), f32),
            pltpu.VMEM((2, half, width), f32),
            pltpu.VMEM((2, tile, width), f32),
            pltpu.SemaphoreType.DMA((6,)),
        ],
        12 * half * tile * width,
        8 * half * tile + 12 * tile * width,
        None if before is None else {5: 0},
    )


def shards(halves, diag_rest, panel_vectors, tri_factor):
    rows, cols = lax.axis_size("row"), lax.axis_size("col")
    routes = Routes(rows, cols)
    at = Place(rows, cols)
    planes, top = routes.planes, routes.top
    half_size, tile_size = halves.shape[1:]
    swap = routes.across_cols(1)
    everyone = [(r, c) for r in range(rows) for c in range(cols)]

    lane = jnp.where(at.apart == 0, 0, half_size)
    arrived = routes.spread(lax.dynamic_slice_in_dim(panel_vectors, lane, half_size, 0))
    partner = routes.send(panel_vectors, swap)

    kept, given, around, cross = row_products(rows, cols, halves, diag_rest, panel_vectors)
    chip_sum = kept + routes.send(given, swap)
    row_sums = []
    for step in range(planes - 1):
        back = [(there, here) for here, there in routes.trips(step)]
        part = jnp.where(at.away == step + 1, chip_sum[:half_size], chip_sum[half_size:])
        row_sums.append(routes.send(part, back))
    home = [(routes.flat(b % rows, b ^ 1), routes.flat(b % rows, b)) for b in range(rows, cols)]
    sum_partner = routes.send(chip_sum, home)

    mine_vec = assemble(rows, cols, panel_vectors, partner, arrived)
    other_vec = routes.send(mine_vec, swap)
    partial = first_column(rows, cols, halves, mine_vec)
    sent, stays, inner = second_column(
        rows, cols, halves, other_vec, panel_vectors, partial, around, cross, chip_sum, sum_partner
    )

    bit = top // 2
    while bit >= 1:
        pairs = [
            (routes.flat(r, c), routes.flat(r ^ bit, c))
            for r, c in everyone
            if (r ^ (c % rows)) & bit and (r ^ (c % rows)) % top // (2 * bit) == 0
        ]
        sent, stays = sent + routes.send(sent, pairs), stays + routes.send(stays, pairs)
        bit //= 2
    lanes = [(r, c) for r, c in everyone if (r ^ (c % rows)) % top == 0]
    total = stays + routes.send(sent, [(routes.flat(r, c), routes.flat(r ^ top, c)) for r, c in lanes])
    for row_sum in row_sums:
        total = total + row_sum

    arrived = routes.spread(total)
    beside = [
        routes.send(total, [(routes.flat(r, c), routes.flat(r ^ step, c)) for r, c in lanes])
        for step in range(1, rows)
    ]

    bit = 1
    while bit < cols:
        inner = inner + routes.send(inner, routes.across_cols(bit))
        bit *= 2
    bit = 1
    while bit < rows:
        inner = inner + routes.send(inner, routes.across_rows(bit))
        bit *= 2

    own_w, half_middle, new_rest = own_w_and_rest(
        rows, cols, panel_vectors, tri_factor, inner, diag_rest, total, beside
    )
    partner_w = routes.send(own_w, swap)
    mine_w = mine_w_panel(rows, cols, mine_vec, tri_factor, half_middle, own_w, partner_w, arrived)
    other_w = routes.send(mine_w, swap)
    updated = update(rows, cols, 0, halves, panel_vectors, own_w, mine_vec, mine_w)
    updated = update(rows, cols, 1, halves, panel_vectors, own_w, other_vec, other_w, updated)
    return (updated, new_rest, own_w)


def solution(mesh):
    return jax.shard_map(
        shards,
        mesh=mesh,
        in_specs=(P(None, "row", "col"), P(("col", "row"), None), P("col", None), P()),
        out_specs=(P(None, "row", "col"), P(("col", "row"), None), P("col", None)),
        check_vma=False,
    )
```
